32 devices in a mesh: dp: 8 (over z, y), fsdp: 4 (over x, core).
Axes of the slice: x: 2, y: 2, z: 4, core: 2. Of those that a mesh axis runs over, the one named last changes fastest.
Arguments:
- tokens: bfloat16 [2, 8192, 1152], P(None, ('dp', 'fsdp')), may hold values from -6 to 6
- condition: bfloat16 [2, 32, 2, 1152], P(None, ('dp', 'fsdp')), may hold values from -6 to 6
- lengths: int32 [2, 32, 2], P(None, ('dp', 'fsdp')), may hold values from 0 to 256, as said below
- w_mod: bfloat16 [1152, 6912], P('fsdp'), may hold values from -0.1875 to 0.1875
- b_mod: float32 [6912], replicated, may hold values from -1.75 to 1.75
- w_qkv: bfloat16 [1152, 3456], P('fsdp'), may hold values from -0.1875 to 0.1875
- b_qkv: float32 [3456], replicated, may hold values from -1.75 to 1.75
- q_gain: float32 [72], replicated, may hold values from 1 to 1.8
- k_gain: float32 [72], replicated, may hold values from 1 to 1.8
- w_o: bfloat16 [1152, 1152], P('fsdp'), may hold values from -0.75 to 0.75
- b_o: float32 [1152], replicated, may hold values from -1.75 to 1.75
- w_gate: bfloat16 [1152, 3072], P('fsdp'), may hold values from -0.1875 to 0.1875
- w_up: bfloat16 [1152, 3072], P('fsdp'), may hold values from -0.1875 to 0.1875
- w_down: bfloat16 [3072, 1152], P('fsdp'), may hold values from -0.109375 to 0.109375
- d_out: bfloat16 [2, 8192, 1152], P(None, ('dp', 'fsdp')), may hold values from -6 to 6
Outputs:
- block_out: bfloat16 [2, 8192, 1152], P(None, ('dp', 'fsdp'))
- d_tokens: float32 [2, 8192, 1152], P(None, ('dp', 'fsdp'))
- d_condition: float32 [2, 32, 2, 1152], P(None, ('dp', 'fsdp'))
- g_mod: float32 [1152, 6912], P('fsdp')
- g_bmod: float32 [6912], replicated
- g_qkv: float32 [1152, 3456], P('fsdp')
- g_bqkv: float32 [3456], replicated
- g_qgain: float32 [72], replicated
- g_kgain: float32 [72], replicated
- g_o: float32 [1152, 1152], P('fsdp')
- g_bo: float32 [1152], replicated
- g_gate: float32 [1152, 3072], P('fsdp')
- g_up: float32 [1152, 3072], P('fsdp')
- g_down: float32 [3072, 1152], P('fsdp')
The draws below stay inside these ranges and needn't reach their ends.
Inputs may be any that keep to these rules, and one draw needn't show every extreme that they name: `lengths`: each packed row of 256 tokens holds either one image of 256 patches in slot 0 (slot 1 empty, length 0) or two images of 128 patches; every image has 16 rows of patches; the first row of every micro-batch holds one image.
All inputs are finite; a program needn't handle non-finite values.
Results may differ from the reference program's by a relative error of at most 0.019.
Values may be sent and summed in bfloat16 or wider, within the bound.
No kernel may reach another device: no remote copies, remote signals or barrier semaphores. Data moves between devices by JAX's collectives and lax.ppermute only.
A program may use at most 320 MiB of HBM per device.

```python
import jax
import jax.numpy as jnp
from jax import lax

D = 1152
HD = 72
FF = 3072
ROWS = 256
GRID_H = 16
MICRO = 2
NROWS = 32
TOKENS = 8192


def draw_lengths(key, part):
    pick = jax.random.randint(key, (MICRO, NROWS), 0, 5)
    first_row = jnp.arange(NROWS, dtype=jnp.int32)[None, :] == 0
    one_big = jnp.logical_or(pick < 3, first_row)
    big_row = jnp.array([ROWS, 0], dtype=jnp.int32)
    small_row = jnp.full((2,), ROWS // 2, dtype=jnp.int32)
    return jnp.where(one_big[:, :, None], big_row[None, None, :], small_row[None, None, :]).astype(jnp.int32)


def level_of(key, dims, split, low, largest):
    level = 1.0
    for axis_at, shards_of in split:
        heights = jax.random.uniform(jax.random.fold_in(jax.random.fold_in(key, 6), axis_at), (shards_of,), jnp.float32, low / len(split), largest / len(split))
        level = level * jnp.repeat(jnp.exp(heights), dims[axis_at] // shards_of).reshape((-1,) + (1,) * (len(dims) - 1 - axis_at))
    return level


def scatter_about(key, extent, width, most, shards=(), held_as=jnp.bfloat16):
    factor_of = level_of(key, extent, shards, -0.22, 0.18) if shards else 1.0
    entries = jax.random.normal(key, extent, jnp.float32) * width * factor_of
    return jnp.minimum(jnp.maximum(entries, -most), most).astype(held_as)


def setup_inputs(seed: int = 0) -> dict:
    seeds = jax.random.split(jax.random.key(seed), 16)
    tokens = scatter_about(seeds[0], (MICRO, TOKENS, D), 1.0, 6.0, ((1, 32),))
    condition = scatter_about(seeds[1], (MICRO, NROWS, 2, D), 1.0, 6.0, ((1, 32),))
    lengths = draw_lengths(jax.random.fold_in(seeds[15], 71), 0)
    w_mod = scatter_about(seeds[3], (D, 6 * D), D ** -0.5, 0.1875, ((0, 4),))
    b_mod = scatter_about(seeds[4], (6 * D,), 0.3, 1.75, (), jnp.float32)
    w_qkv = scatter_about(seeds[5], (D, 3 * D), D ** -0.5, 0.1875, ((0, 4),))
    b_qkv = scatter_about(seeds[6], (3 * D,), 0.3, 1.75, (), jnp.float32)
    q_gain = jnp.clip(jax.random.uniform(seeds[7], (HD,), jnp.float32, 1.0, 1.8), 1.0, 1.8)
    k_gain = jnp.clip(jax.random.uniform(seeds[8], (HD,), jnp.float32, 1.0, 1.8), 1.0, 1.8)
    w_o = scatter_about(seeds[9], (D, D), (D // 16) ** -0.5, 0.75, ((0, 4),))
    b_o = scatter_about(seeds[10], (D,), 0.3, 1.75, (), jnp.float32)
    w_gate = scatter_about(seeds[11], (D, FF), D ** -0.5, 0.1875, ((0, 4),))
    w_up = scatter_about(seeds[12], (D, FF), D ** -0.5, 0.1875, ((0, 4),))
    w_down = scatter_about(seeds[13], (FF, D), FF ** -0.5, 0.109375, ((0, 4),))
    d_out = scatter_about(seeds[14], (MICRO, TOKENS, D), 1.0, 6.0, ((1, 32),))
    return {"tokens": tokens, "condition": condition, "lengths": lengths, "w_mod": w_mod, "b_mod": b_mod, "w_qkv": w_qkv, "b_qkv": b_qkv, "q_gain": q_gain, "k_gain": k_gain, "w_o": w_o, "b_o": b_o, "w_gate": w_gate, "w_up": w_up, "w_down": w_down, "d_out": d_out}


@jax.custom_vjp
def low(v):
    return lax.optimization_barrier(v.astype(jnp.bfloat16)).astype(jnp.float32)

@jax.custom_vjp
def low_back(v):
    return v

def low_keep(v):
    return (low(v), None)

def low_pass(kept, grad):
    return (grad,)

def back_keep(v):
    return (v, None)

def back_low(kept, grad):
    return (low(grad),)
low.defvjp(low_keep, low_pass)
low_back.defvjp(back_keep, back_low)
EPSILON = 1e-06
MASKED = -1e+30

def mat_mul(left, right):
    return jnp.dot(left, right, precision=lax.Precision.HIGHEST)

def pack_layout(lengths_row, row_count):
    slot_count = lengths_row.shape[0]
    slot_ends = jnp.cumsum(lengths_row).astype(jnp.int32)
    slot_starts = (slot_ends - lengths_row).astype(jnp.int32)
    tok_index = jnp.arange(row_count, dtype=jnp.int32)
    segment = lax.optimization_barrier(jnp.sum((tok_index[:, None] >= slot_ends[None, :slot_count - 1]).astype(jnp.int32), axis=1)).astype(jnp.int32)
    slot_ids = jnp.arange(slot_count, dtype=jnp.int32)
    member = segment[:, None] == slot_ids[None, :]
    offset = lax.optimization_barrier(jnp.sum(jnp.where(member, slot_starts[None, :], 0), axis=1)).astype(jnp.int32)
    widths = jnp.maximum(lengths_row // GRID_H, 1).astype(jnp.int32)
    tok_width = lax.optimization_barrier(jnp.sum(jnp.where(member, widths[None, :], 0), axis=1)).astype(jnp.int32)
    position = (tok_index - offset).astype(jnp.int32)
    return (segment, member.astype(jnp.float32), position // tok_width, position % tok_width)

def rope_angles(grid_row, grid_col, head_dim):
    quarter = head_dim // 4
    frequency = 10000.0 ** (-jnp.arange(quarter, dtype=jnp.float32) / quarter)
    angle_table = jnp.concatenate([grid_row.astype(jnp.float32)[:, None] * frequency[None, :], grid_col.astype(jnp.float32)[:, None] * frequency[None, :]], axis=1)
    return (jnp.cos(angle_table)[:, None, :], jnp.sin(angle_table)[:, None, :])

def norm_mod(field, scale_part, shift_part):
    inverse = lax.rsqrt(lax.optimization_barrier(jnp.mean(field * field, axis=-1, keepdims=True)) + EPSILON)
    return field * inverse * (1.0 + scale_part) + shift_part

def rotate(vector, cosine, sine_table):
    half_dim = vector.shape[-1] // 2
    first = vector[..., :half_dim]
    second = vector[..., half_dim:]
    return jnp.concatenate([first * cosine - second * sine_table, second * cosine + first * sine_table], axis=-1)

def head_prep(cosine, sine_table, raw_head, gain_vec):
    inverse = lax.rsqrt(lax.optimization_barrier(jnp.mean(raw_head * raw_head, axis=-1, keepdims=True)) + EPSILON)
    return rotate(raw_head * inverse * gain_vec, cosine, sine_table)

def row_forward(row_tokens, row_cond, row_lengths, w_mod, b_mod, w_qkv, b_qkv, q_gain, k_gain, w_o, b_o, w_gate, w_up, w_down):
    row_count, model_width = row_tokens.shape
    head_dim = q_gain.shape[0]
    head_count = model_width // head_dim
    segment, member, grid_row, grid_col = pack_layout(row_lengths, row_count)
    cosine, sine_table = rope_angles(grid_row, grid_col, head_dim)
    silu_cond = low(jax.nn.silu(row_cond))
    mod_slots = low_back(mat_mul(silu_cond, w_mod)) + b_mod
    mod_tokens = mat_mul(member, mod_slots)
    mod_parts = [mod_tokens[:, slot_part * model_width:(slot_part + 1) * model_width] for slot_part in range(6)]
    norm_one = low(norm_mod(row_tokens, mod_parts[1], mod_parts[0]))
    qkv_all = low_back(mat_mul(norm_one, w_qkv)) + b_qkv
    q_raw = qkv_all[:, :model_width].reshape(row_count, head_count, head_dim)
    k_raw = qkv_all[:, model_width:2 * model_width].reshape(row_count, head_count, head_dim)
    v_raw = qkv_all[:, 2 * model_width:].reshape(row_count, head_count, head_dim)
    q_rot = low(head_prep(cosine, sine_table, q_raw, q_gain))
    k_rot = low(head_prep(cosine, sine_table, k_raw, k_gain))
    v_low = low(v_raw)
    same_slot = segment[:, None] == segment[None, :]
    raw_score = low_back(jnp.einsum('qhd,khd->hqk', q_rot, k_rot, precision=lax.Precision.HIGHEST))
    score = jnp.where(same_slot[None, :, :], raw_score * head_dim ** (-0.5), MASKED)
    attn_prob = jax.nn.softmax(score, axis=-1)
    attn_mix = jnp.einsum('hqk,khd->qhd', low(attn_prob), v_low, precision=lax.Precision.HIGHEST)
    attn_out = low(low_back(attn_mix)).reshape(row_count, model_width)
    branch = low_back(mat_mul(attn_out, w_o)) + b_o
    res_one = row_tokens + mod_parts[2] * branch
    norm_two = low(norm_mod(res_one, mod_parts[4], mod_parts[3]))
    gate_pre = low_back(mat_mul(norm_two, w_gate))
    up_pre = low_back(mat_mul(norm_two, w_up))
    hidden = low(jax.nn.silu(gate_pre) * up_pre)
    mlp_out = low_back(mat_mul(hidden, w_down))
    return res_one + mod_parts[5] * mlp_out

def reference(tokens, condition, lengths, w_mod, b_mod, w_qkv, b_qkv, q_gain, k_gain, w_o, b_o, w_gate, w_up, w_down, d_out):
    params = tuple((param_value.astype(jnp.float32) for param_value in (w_mod, b_mod, w_qkv, b_qkv, q_gain, k_gain, w_o, b_o, w_gate, w_up, w_down)))
    model_width = tokens.shape[2]
    slot_count = condition.shape[2]
    row_total = tokens.shape[0] * (tokens.shape[1] // ROWS)
    flat_tokens = tokens.astype(jnp.float32).reshape(row_total, ROWS, model_width)
    flat_cond = condition.astype(jnp.float32).reshape(row_total, slot_count, model_width)
    flat_lengths = lengths.reshape(row_total, slot_count).astype(jnp.int32)
    flat_grad = d_out.astype(jnp.float32).reshape(row_total, ROWS, model_width)

    def row_step(grad_carry, row_item):
        row_tokens, row_cond, row_lengths, row_grad = row_item

        def row_fn(tok_arg, cond_arg, *weight_args):
            return row_forward(tok_arg, cond_arg, row_lengths, *weight_args)
        row_out, pullback = jax.vjp(row_fn, row_tokens, row_cond, *params)
        row_grads = pullback(row_grad)
        new_carry = tuple((before_sum + row_term for before_sum, row_term in zip(grad_carry, row_grads[2:])))
        return (new_carry, (row_out.astype(jnp.bfloat16), row_grads[0], row_grads[1]))
    zero_carry = tuple((jnp.zeros(param_item.shape, jnp.float32) for param_item in params))
    final_carry, stacked = lax.scan(row_step, zero_carry, (flat_tokens, flat_cond, flat_lengths, flat_grad))
    block_out = stacked[0].reshape(tokens.shape)
    d_tokens = stacked[1].reshape(tokens.shape)
    d_condition = stacked[2].reshape(condition.shape)
    return (block_out, d_tokens, d_condition, final_carry[0], final_carry[1], final_carry[2], final_carry[3], final_carry[4], final_carry[5], final_carry[6], final_carry[7], final_carry[8], final_carry[9], final_carry[10])
```

```python
from functools import partial

import jax
import jax.numpy as jnp
from jax import lax
from jax.sharding import PartitionSpec as P

GRID_H = 16
EPSILON = 1e-06
MASKED = -1e30
AXES = ("dp", "fsdp")
BF = jnp.bfloat16
F32 = jnp.float32


def bmm(left, right):
    return jnp.dot(left, right, preferred_element_type=F32)


def silu_grad(values):
    sigmoid = jax.nn.sigmoid(values)
    return sigmoid * (1.0 + values * (1.0 - sigmoid))


def pack_layout(lengths_row, row_count):
    slot_ends = jnp.cumsum(lengths_row)
    tok_index = jnp.arange(row_count, dtype=jnp.int32)
    second = tok_index >= slot_ends[0]
    offset = jnp.where(second, slot_ends[0], 0)
    widths = jnp.maximum(lengths_row // GRID_H, 1)
    tok_width = jnp.where(second, widths[1], widths[0])
    position = tok_index - offset
    return second, position // tok_width, position % tok_width


def rope_angles(grid_row, grid_col, head_dim):
    quarter = head_dim // 4
    frequency = 10000.0 ** (-jnp.arange(quarter, dtype=F32) / quarter)
    angle_table = jnp.concatenate(
        [
            grid_row.astype(F32)[..., None] * frequency,
            grid_col.astype(F32)[..., None] * frequency,
        ],
        axis=-1,
    )
    return jnp.cos(angle_table)[..., None, :], jnp.sin(angle_table)[..., None, :]


def norm_mod(field, scale_part, shift_part):
    inverse = lax.rsqrt(jnp.mean(field * field, axis=-1, keepdims=True) + EPSILON)
    return field * inverse * (1.0 + scale_part) + shift_part


def norm_mod_back(field, scale_part, grad):
    inverse = lax.rsqrt(jnp.mean(field * field, axis=-1, keepdims=True) + EPSILON)
    normed = field * inverse
    scaled = grad * (1.0 + scale_part)
    d_field = inverse * (scaled - normed * jnp.mean(scaled * normed, axis=-1, keepdims=True))
    return d_field, grad * normed


def rotate(vector, cosine, sine_table):
    half_dim = vector.shape[-1] // 2
    first = vector[..., :half_dim]
    second = vector[..., half_dim:]
    return jnp.concatenate(
        [first * cosine - second * sine_table, second * cosine + first * sine_table], axis=-1
    )


def head_prep(cosine, sine_table, raw_head, gain_vec):
    inverse = lax.rsqrt(jnp.mean(raw_head * raw_head, axis=-1, keepdims=True) + EPSILON)
    return rotate(raw_head * inverse * gain_vec, cosine, sine_table)


class Cube:
    def __init__(self, dp, fsdp):
        self.total = dp * fsdp
        self.fsdp = fsdp
        me_f = lax.axis_index("fsdp")
        me_d = lax.axis_index("dp")
        self.f = me_f
        self.core = me_f % 2
        self.x = me_f // 2
        self.y = me_d % 2
        self.z0 = (me_d // 2) % 2

    def swap(self, value, mask):
        pairs = [(i, i ^ mask) for i in range(self.total)]
        return lax.ppermute(value, AXES, pairs)


CORE, XBIT, YBIT, Z0BIT, Z1BIT = 1, 2, 4, 8, 16
STAGES = (CORE, XBIT, YBIT, Z0BIT, Z1BIT)


def pick(value, index):
    return lax.dynamic_index_in_dim(value, index, 0, keepdims=False)


def place(parts, bit):
    own, other = parts
    base = jnp.stack([own, own])
    return lax.dynamic_update_index_in_dim(base, other, 1 - bit, 0)


def gather_matrix(cube, shard, gate):
    rows, cols = shard.shape
    if gate is not None:
        shard, _ = lax.optimization_barrier((shard, gate))
    half = lax.dynamic_slice_in_dim(shard, cube.y * (rows // 2), rows // 2, 0)
    got_x = cube.swap(half, XBIT)
    got_c = cube.swap(shard, CORE)
    got_y = cube.swap(got_x, YBIT)
    far_x = cube.swap(got_x, CORE)
    far_y = cube.swap(got_y, CORE)
    full = jnp.zeros((4 * rows, cols), shard.dtype)

    def put(full, value, start):
        return lax.dynamic_update_slice_in_dim(full, value, start, 0)

    other = cube.f ^ 2
    far = cube.f ^ 3
    step = rows // 2
    full = put(full, shard, cube.f * rows)
    full = put(full, got_c, (cube.f ^ 1) * rows)
    full = put(full, got_x, other * rows + cube.y * step)
    full = put(full, got_y, other * rows + (1 - cube.y) * step)
    full = put(full, far_x, far * rows + cube.y * step)
    full = put(full, far_y, far * rows + (1 - cube.y) * step)
    return full, got_x


def reduce_matrix(cube, grad):
    rows = grad.shape[0] // 4
    cols = grad.shape[1]
    view = grad.reshape(2, 2, rows, cols)
    keep = lax.dynamic_index_in_dim(view, cube.core, 1, keepdims=False)
    send = lax.dynamic_index_in_dim(view, 1 - cube.core, 1, keepdims=False)
    view = keep + cube.swap(send, CORE)
    view = pick(view, cube.x) + cube.swap(pick(view, 1 - cube.x), XBIT)
    view = view.reshape(2, rows // 2, cols)
    view = pick(view, cube.y) + cube.swap(pick(view, 1 - cube.y), YBIT)
    view = view.reshape(2, rows // 4, cols)
    view = pick(view, cube.z0) + cube.swap(pick(view, 1 - cube.z0), Z0BIT)
    total = view + cube.swap(view, Z1BIT)
    pair = place((total, cube.swap(total, Z0BIT)), cube.z0).reshape(rows // 2, cols)
    both = place((pair, cube.swap(pair, YBIT)), cube.y).reshape(rows, cols)
    return both.astype(F32)


def gather_rows(cube, value):
    for mask in STAGES:
        value = jnp.concatenate([value, cube.swap(value, mask)], axis=0)
    return value


def sum_all(cube, value):
    for mask in STAGES:
        value = value + cube.swap(value, mask)
    return value


def shards_fast(
    tokens, condition, lengths, w_mod, b_mod, w_qkv, b_qkv, q_gain, k_gain, w_o, b_o,
    w_gate, w_up, w_down, d_out, *, dp, fsdp
):
    cube = Cube(dp, fsdp)
    micro_count, row_count, width = tokens.shape
    slot_count = condition.shape[2]
    slots = micro_count * slot_count
    head_dim = q_gain.shape[0]
    heads = width // head_dim
    count = micro_count * row_count
    shard_rows = w_mod.shape[0]

    cond = condition.reshape(slots, width).astype(F32)
    silu_cond = jax.nn.silu(cond).astype(BF)
    near = [silu_cond] + [cube.swap(silu_cond, mask) for mask in (1, 2, 3)]
    near_cond = jnp.concatenate(near, axis=0)
    mine = lax.dynamic_slice_in_dim(near_cond, cube.f * shard_rows, shard_rows, 1)
    part = bmm(mine, w_mod).reshape(fsdp, slots, -1)
    mod = part[0] + b_mod
    for mask in (1, 2, 3):
        mod = mod + cube.swap(part[mask], mask)
    all_cond = near_cond
    for mask in (YBIT, Z0BIT, Z1BIT):
        all_cond = jnp.concatenate([all_cond, cube.swap(all_cond, mask)], axis=0)
    all_cond = lax.dynamic_slice_in_dim(all_cond, cube.f * shard_rows, shard_rows, 1)

    full_qkv, gate_a = gather_matrix(cube, w_qkv, None)
    full_o, gate_b = gather_matrix(cube, w_o, None)
    full_gate, gate_c = gather_matrix(cube, w_gate, gate_a)
    full_up, gate_d = gather_matrix(cube, w_up, gate_b)
    full_down, gate_e = gather_matrix(cube, w_down, gate_c)

    second, grid_row, grid_col = jax.vmap(lambda item: pack_layout(item, row_count))(
        lengths.reshape(micro_count, slot_count)
    )
    cosine, sine_table = rope_angles(grid_row, grid_col, head_dim)
    mod = mod.reshape(micro_count, slot_count, 6, width)
    mod_parts = [
        jnp.where(second[:, :, None], mod[:, 1, None, i], mod[:, 0, None, i]) for i in range(6)
    ]
    shift1, scale1, gate1, shift2, scale2, gate2 = [
        item.reshape(count, width) for item in mod_parts
    ]
    tok = tokens.reshape(count, width).astype(F32)
    row_grad = d_out.reshape(count, width).astype(F32)
    norm_one = norm_mod(tok, scale1, shift1).astype(BF)
    qkv_all = bmm(norm_one, full_qkv) + b_qkv
    shape4 = (micro_count, row_count, heads, head_dim)
    q_raw = qkv_all[:, :width].reshape(shape4)
    k_raw = qkv_all[:, width : 2 * width].reshape(shape4)
    v_low = qkv_all[:, 2 * width :].reshape(shape4).astype(BF)
    q_rot = head_prep(cosine, sine_table, q_raw, q_gain).astype(BF)
    k_rot = head_prep(cosine, sine_table, k_raw, k_gain).astype(BF)
    same_slot = second[:, :, None] == second[:, None, :]
    scale = head_dim ** (-0.5)
    raw = jnp.einsum("mqhd,mkhd->mhqk", q_rot, k_rot, preferred_element_type=F32)
    score = jnp.where(same_slot[:, None], raw * scale, MASKED)
    top = jnp.max(score, axis=-1, keepdims=True)
    log_total = top + jnp.log(jnp.sum(jnp.exp(score - top), axis=-1, keepdims=True))
    prob = jnp.exp(score - log_total)
    attn = jnp.einsum("mhqk,mkhd->mqhd", prob.astype(BF), v_low, preferred_element_type=F32)
    attn = attn.astype(BF).reshape(count, width)
    branch = bmm(attn, full_o) + b_o
    res_one = tok + gate1 * branch
    norm_two = norm_mod(res_one, scale2, shift2).astype(BF)
    gate_pre = bmm(norm_two, full_gate)
    up_pre = bmm(norm_two, full_up)
    hidden = (jax.nn.silu(gate_pre) * up_pre).astype(BF)
    mlp_out = bmm(hidden, full_down)
    block_out = (res_one + gate2 * mlp_out).astype(BF)

    d_mlp = (row_grad * gate2).astype(BF)
    d_gate2 = row_grad * mlp_out
    g_down = reduce_matrix(cube, bmm(hidden.T, d_mlp).astype(BF))
    d_hidden = bmm(d_mlp, full_down.T)
    d_gate = (d_hidden * up_pre * silu_grad(gate_pre)).astype(BF)
    d_upper = (d_hidden * jax.nn.silu(gate_pre)).astype(BF)
    g_gate = reduce_matrix(cube, bmm(norm_two.T, d_gate).astype(BF))
    g_up = reduce_matrix(cube, bmm(norm_two.T, d_upper).astype(BF))
    d_norm_two = bmm(d_gate, full_gate.T) + bmm(d_upper, full_up.T)
    d_res_norm, d_scale2 = norm_mod_back(res_one, scale2, d_norm_two)
    d_res_one = row_grad + d_res_norm
    d_branch = d_res_one * gate1
    d_gate1 = d_res_one * branch
    g_bo = jnp.sum(d_branch, axis=0)
    d_proj = d_branch.astype(BF)
    g_o = reduce_matrix(cube, bmm(attn.T, d_proj).astype(BF))
    d_attn = bmm(d_proj, full_o.T).astype(BF).reshape(shape4)
    d_prob = jnp.einsum("mqhd,mkhd->mhqk", d_attn, v_low, preferred_element_type=F32)
    d_value = jnp.einsum("mhqk,mqhd->mkhd", prob.astype(BF), d_attn, preferred_element_type=F32)
    row_dot = jnp.sum(prob * d_prob, axis=-1, keepdims=True)
    d_score = (prob * (d_prob - row_dot) * scale).astype(BF)
    d_q_rot = jnp.einsum("mhqk,mkhd->mqhd", d_score, k_rot, preferred_element_type=F32)
    d_k_rot = jnp.einsum("mhqk,mqhd->mkhd", d_score, q_rot, preferred_element_type=F32)
    prep_fn = partial(head_prep, cosine, sine_table)
    _, back_query = jax.vjp(prep_fn, q_raw, q_gain)
    d_query, g_qgain = back_query(d_q_rot)
    _, back_key = jax.vjp(prep_fn, k_raw, k_gain)
    d_key, g_kgain = back_key(d_k_rot)
    d_qkv = jnp.concatenate(
        [d_query.reshape(count, width), d_key.reshape(count, width), d_value.reshape(count, width)],
        axis=1,
    )
    g_bqkv = jnp.sum(d_qkv, axis=0)
    d_qkv_low = d_qkv.astype(BF)
    g_qkv = reduce_matrix(cube, bmm(norm_one.T, d_qkv_low).astype(BF))
    d_norm_one = bmm(d_qkv_low, full_qkv.T)
    d_tok_norm, d_scale1 = norm_mod_back(tok, scale1, d_norm_one)
    d_tokens = d_res_one + d_tok_norm

    member = jnp.stack([1.0 - second.astype(F32), second.astype(F32)], axis=1)

    def slot_sums(value):
        grouped = value.reshape(micro_count, row_count, width)
        first = jnp.sum(grouped * member[:, 0, :, None], axis=1)
        other = jnp.sum(grouped * member[:, 1, :, None], axis=1)
        return jnp.stack([first, other], axis=1).reshape(slots, width)

    d_mod = jnp.concatenate(
        [slot_sums(item) for item in (d_norm_one, d_scale1, d_gate1, d_norm_two, d_scale2, d_gate2)],
        axis=1,
    )
    d_mod_low = d_mod.astype(BF)
    all_mod = gather_rows(cube, d_mod_low)
    g_mod = bmm(all_cond.T, all_mod)
    back = lax.dot_general(
        all_mod[: fsdp * slots], w_mod, (((1,), (1,)), ((), ())), preferred_element_type=F32
    ).reshape(fsdp, slots, shard_rows)
    parts = [back[0]] + [cube.swap(back[mask], mask) for mask in (1, 2, 3)]
    stacked = jnp.stack(parts, axis=0)
    order = jnp.arange(fsdp, dtype=jnp.int32) ^ cube.f
    d_cond = jnp.take(stacked, order, axis=0)
    d_cond = jnp.transpose(d_cond, (1, 0, 2)).reshape(slots, width) * silu_grad(cond)

    minor = jnp.concatenate([jnp.sum(d_mod, axis=0), g_bqkv, g_bo, g_qgain, g_kgain])
    minor = sum_all(cube, minor)
    edges = [0, 6 * width, 9 * width, 10 * width, 10 * width + head_dim, 10 * width + 2 * head_dim]
    g_bmod, g_bqkv, g_bo, g_qgain, g_kgain = [
        minor[low:high] for low, high in zip(edges[:-1], edges[1:])
    ]
    return (
        block_out.reshape(tokens.shape),
        d_tokens.reshape(tokens.shape),
        d_cond.reshape(condition.shape),
        g_mod,
        g_bmod,
        g_qkv,
        g_bqkv,
        g_qgain,
        g_kgain,
        g_o,
        g_bo,
        g_gate,
        g_up,
        g_down,
    )


def plain_layout(lengths_row, row_count):
    second, grid_row, grid_col = pack_layout(lengths_row, row_count)
    segment = second.astype(jnp.int32)
    slot_ids = jnp.arange(lengths_row.shape[0], dtype=jnp.int32)
    member = segment[:, None] == slot_ids[None, :]
    return segment, member.astype(jnp.float32), grid_row, grid_col


def score_block(q_rot, k_rot, same_slot, score_scale):
    raw_score = jnp.einsum("qhd,khd->hqk", q_rot, k_rot, preferred_element_type=jnp.float32)
    return jnp.where(same_slot[None, :, :], raw_score * score_scale, MASKED)


def forward(row_tokens, row_cond, row_lengths, matrices, minor_params):
    w_mod, w_qkv, w_o, w_gate, w_up, w_down = matrices
    b_mod, b_qkv, q_gain, k_gain, b_o = minor_params
    row_count, model_width = row_tokens.shape
    head_dim = q_gain.shape[0]
    head_count = model_width // head_dim
    segment, member, grid_row, grid_col = plain_layout(row_lengths, row_count)
    cosine, sine_table = rope_angles(grid_row, grid_col, head_dim)
    cond_float = row_cond.astype(jnp.float32)
    silu_cond = jax.nn.silu(cond_float).astype(jnp.bfloat16)
    mod_slots = jnp.dot(silu_cond, w_mod, preferred_element_type=jnp.float32) + b_mod
    mod_tokens = jnp.dot(member, mod_slots, precision=lax.Precision.HIGHEST)
    mod_parts = [
        mod_tokens[:, slot_part * model_width : (slot_part + 1) * model_width]
        for slot_part in range(6)
    ]
    tok_float = row_tokens.astype(jnp.float32)
    norm_one = norm_mod(tok_float, mod_parts[1], mod_parts[0]).astype(jnp.bfloat16)
    qkv_all = jnp.dot(norm_one, w_qkv, preferred_element_type=jnp.float32) + b_qkv
    q_raw = qkv_all[:, :model_width].reshape(row_count, head_count, head_dim)
    k_raw = qkv_all[:, model_width : 2 * model_width].reshape(row_count, head_count, head_dim)
    v_low = (
        qkv_all[:, 2 * model_width :].reshape(row_count, head_count, head_dim).astype(jnp.bfloat16)
    )
    q_rot = head_prep(cosine, sine_table, q_raw, q_gain).astype(jnp.bfloat16)
    k_rot = head_prep(cosine, sine_table, k_raw, k_gain).astype(jnp.bfloat16)
    same_slot = segment[:, None] == segment[None, :]
    score_scale = head_dim ** (-0.5)
    score = score_block(q_rot, k_rot, same_slot, score_scale)
    top_score = jnp.max(score, axis=-1, keepdims=True)
    log_total = top_score + jnp.log(jnp.sum(jnp.exp(score - top_score), axis=-1, keepdims=True))
    attn_prob = jnp.exp(score - log_total)
    attn_out = jnp.einsum(
        "hqk,khd->qhd", attn_prob.astype(jnp.bfloat16), v_low, preferred_element_type=jnp.float32
    )
    attn_out = attn_out.astype(jnp.bfloat16).reshape(row_count, model_width)
    branch = jnp.dot(attn_out, w_o, preferred_element_type=jnp.float32) + b_o
    res_one = tok_float + mod_parts[2] * branch
    norm_two = norm_mod(res_one, mod_parts[4], mod_parts[3]).astype(jnp.bfloat16)
    gate_pre = jnp.dot(norm_two, w_gate, preferred_element_type=jnp.float32)
    up_pre = jnp.dot(norm_two, w_up, preferred_element_type=jnp.float32)
    hidden = (jax.nn.silu(gate_pre) * up_pre).astype(jnp.bfloat16)
    mlp_out = jnp.dot(hidden, w_down, preferred_element_type=jnp.float32)
    block_row = res_one + mod_parts[5] * mlp_out
    stored = {
        "member": member,
        "cosine": cosine,
        "sine_table": sine_table,
        "cond_float": cond_float,
        "silu_cond": silu_cond,
        "mod_parts": mod_parts,
        "tok_float": tok_float,
        "norm_one": norm_one,
        "q_raw": q_raw,
        "k_raw": k_raw,
        "q_rot": q_rot,
        "k_rot": k_rot,
        "v_low": v_low,
        "same_slot": same_slot,
        "log_total": log_total,
        "attn_out": attn_out,
        "branch": branch,
        "res_one": res_one,
        "norm_two": norm_two,
        "gate_pre": gate_pre,
        "up_pre": up_pre,
        "hidden": hidden,
        "mlp_out": mlp_out,
    }
    return (block_row, stored)


def backward(stored, row_grad, matrices, minor_params):
    w_mod, w_qkv, w_o, w_gate, w_up, w_down = matrices
    b_mod, b_qkv, q_gain, k_gain, b_o = minor_params
    row_count, model_width = row_grad.shape
    head_dim = q_gain.shape[0]
    head_count = model_width // head_dim
    score_scale = head_dim ** (-0.5)
    mod_parts = stored["mod_parts"]
    d_mlp = (row_grad * mod_parts[5]).astype(jnp.bfloat16)
    d_gate2 = row_grad * stored["mlp_out"]
    g_down = jnp.dot(stored["hidden"].T, d_mlp, preferred_element_type=jnp.float32)
    d_hidden = jnp.dot(d_mlp, w_down.T, preferred_element_type=jnp.float32)
    gate_pre = stored["gate_pre"]
    d_gate = (d_hidden * stored["up_pre"] * silu_grad(gate_pre)).astype(jnp.bfloat16)
    d_upper = (d_hidden * jax.nn.silu(gate_pre)).astype(jnp.bfloat16)
    g_gate = jnp.dot(stored["norm_two"].T, d_gate, preferred_element_type=jnp.float32)
    g_up = jnp.dot(stored["norm_two"].T, d_upper, preferred_element_type=jnp.float32)
    d_norm_two = jnp.dot(d_gate, w_gate.T, preferred_element_type=jnp.float32) + jnp.dot(
        d_upper, w_up.T, preferred_element_type=jnp.float32
    )
    unused_two, back_two = jax.vjp(norm_mod, stored["res_one"], mod_parts[4], mod_parts[3])
    d_res_norm, d_scale2, d_shift2 = back_two(d_norm_two)
    d_res_one = row_grad + d_res_norm
    d_branch = d_res_one * mod_parts[2]
    d_gate1 = d_res_one * stored["branch"]
    g_bo = jnp.sum(d_branch, axis=0)
    d_proj = d_branch.astype(jnp.bfloat16)
    g_o = jnp.dot(stored["attn_out"].T, d_proj, preferred_element_type=jnp.float32)
    d_attn = (
        jnp.dot(d_proj, w_o.T, preferred_element_type=jnp.float32)
        .astype(jnp.bfloat16)
        .reshape(row_count, head_count, head_dim)
    )
    q_rot = stored["q_rot"]
    k_rot = stored["k_rot"]
    v_low = stored["v_low"]
    score = score_block(q_rot, k_rot, stored["same_slot"], score_scale)
    attn_prob = jnp.exp(score - stored["log_total"])
    d_prob = jnp.einsum("qhd,khd->hqk", d_attn, v_low, preferred_element_type=jnp.float32)
    d_value = jnp.einsum(
        "hqk,qhd->khd", attn_prob.astype(jnp.bfloat16), d_attn, preferred_element_type=jnp.float32
    )
    row_dot = jnp.sum(attn_prob * d_prob, axis=-1, keepdims=True)
    d_score = (attn_prob * (d_prob - row_dot) * score_scale).astype(jnp.bfloat16)
    d_q_rot = jnp.einsum("hqk,khd->qhd", d_score, k_rot, preferred_element_type=jnp.float32)
    d_k_rot = jnp.einsum("hqk,qhd->khd", d_score, q_rot, preferred_element_type=jnp.float32)
    prep_fn = partial(head_prep, stored["cosine"], stored["sine_table"])
    unused_q, back_query = jax.vjp(prep_fn, stored["q_raw"], q_gain)
    d_query, g_qgain = back_query(d_q_rot)
    unused_k, back_key = jax.vjp(prep_fn, stored["k_raw"], k_gain)
    d_key, g_kgain = back_key(d_k_rot)
    d_qkv = jnp.concatenate(
        [
            d_query.reshape(row_count, model_width),
            d_key.reshape(row_count, model_width),
            d_value.reshape(row_count, model_width),
        ],
        axis=1,
    )
    g_bqkv = jnp.sum(d_qkv, axis=0)
    d_qkv_low = d_qkv.astype(jnp.bfloat16)
    g_qkv = jnp.dot(stored["norm_one"].T, d_qkv_low, preferred_element_type=jnp.float32)
    d_norm_one = jnp.dot(d_qkv_low, w_qkv.T, preferred_element_type=jnp.float32)
    unused_one, back_one = jax.vjp(norm_mod, stored["tok_float"], mod_parts[1], mod_parts[0])
    d_tok_norm, d_scale1, d_shift1 = back_one(d_norm_one)
    d_tokens = d_res_one + d_tok_norm
    d_mod_tokens = jnp.concatenate(
        [d_shift1, d_scale1, d_gate1, d_shift2, d_scale2, d_gate2], axis=1
    )
    d_mod = jnp.dot(stored["member"].T, d_mod_tokens, precision=lax.Precision.HIGHEST)
    g_bmod = jnp.sum(d_mod, axis=0)
    d_mod_low = d_mod.astype(jnp.bfloat16)
    g_mod = jnp.dot(stored["silu_cond"].T, d_mod_low, preferred_element_type=jnp.float32)
    d_condition = jnp.dot(d_mod_low, w_mod.T, preferred_element_type=jnp.float32) * silu_grad(
        stored["cond_float"]
    )
    return (
        d_tokens,
        d_condition,
        (g_mod, g_qkv, g_o, g_gate, g_up, g_down),
        (g_bmod, g_bqkv, g_qgain, g_kgain, g_bo),
    )


def sum_data(grad_parts):
    return (
        lax.psum(grad_parts[0].astype(jnp.bfloat16), "dp").astype(jnp.float32),
        lax.psum(grad_parts[1].astype(jnp.bfloat16), "dp").astype(jnp.float32),
        lax.psum(grad_parts[2].astype(jnp.bfloat16), "dp").astype(jnp.float32),
        lax.psum(grad_parts[3].astype(jnp.bfloat16), "dp").astype(jnp.float32),
        lax.psum(grad_parts[4].astype(jnp.bfloat16), "dp").astype(jnp.float32),
        lax.psum(grad_parts[5].astype(jnp.bfloat16), "dp").astype(jnp.float32),
    )


def add_parts(first_parts, second_parts):
    return tuple(
        (left_part + right_part for left_part, right_part in zip(first_parts, second_parts))
    )


def shards_plain(
    tokens,
    condition,
    lengths,
    w_mod,
    b_mod,
    w_qkv,
    b_qkv,
    q_gain,
    k_gain,
    w_o,
    b_o,
    w_gate,
    w_up,
    w_down,
    d_out,
):
    minor_params = (b_mod, b_qkv, q_gain, k_gain, b_o)
    micro_count = tokens.shape[0]
    out_rows = []
    grad_rows = []
    cond_rows = []
    shard_total = None
    minor_total = None
    for micro in range(micro_count):
        matrices = (
            lax.all_gather(w_mod, "fsdp", axis=0, tiled=True),
            lax.all_gather(w_qkv, "fsdp", axis=0, tiled=True),
            lax.all_gather(w_o, "fsdp", axis=0, tiled=True),
            lax.all_gather(w_gate, "fsdp", axis=0, tiled=True),
            lax.all_gather(w_up, "fsdp", axis=0, tiled=True),
            lax.all_gather(w_down, "fsdp", axis=0, tiled=True),
        )
        block_row, stored = forward(
            tokens[micro], condition[micro, 0], lengths[micro, 0], matrices, minor_params
        )
        out_rows.append(block_row.astype(jnp.bfloat16))
        back_matrices = (
            lax.all_gather(w_mod, "fsdp", axis=0, tiled=True),
            lax.all_gather(w_qkv, "fsdp", axis=0, tiled=True),
            lax.all_gather(w_o, "fsdp", axis=0, tiled=True),
            lax.all_gather(w_gate, "fsdp", axis=0, tiled=True),
            lax.all_gather(w_up, "fsdp", axis=0, tiled=True),
            lax.all_gather(w_down, "fsdp", axis=0, tiled=True),
        )
        d_row, d_cond_row, full_grads, minor_grads = backward(
            stored, d_out[micro].astype(jnp.float32), back_matrices, minor_params
        )
        grad_rows.append(d_row)
        cond_rows.append(d_cond_row[None, :, :])
        shard_grads = (
            lax.psum_scatter(
                full_grads[0].astype(jnp.bfloat16), "fsdp", scatter_dimension=0, tiled=True
            ).astype(jnp.float32),
            lax.psum_scatter(
                full_grads[1].astype(jnp.bfloat16), "fsdp", scatter_dimension=0, tiled=True
            ).astype(jnp.float32),
            lax.psum_scatter(
                full_grads[2].astype(jnp.bfloat16), "fsdp", scatter_dimension=0, tiled=True
            ).astype(jnp.float32),
            lax.psum_scatter(
                full_grads[3].astype(jnp.bfloat16), "fsdp", scatter_dimension=0, tiled=True
            ).astype(jnp.float32),
            lax.psum_scatter(
                full_grads[4].astype(jnp.bfloat16), "fsdp", scatter_dimension=0, tiled=True
            ).astype(jnp.float32),
            lax.psum_scatter(
                full_grads[5].astype(jnp.bfloat16), "fsdp", scatter_dimension=0, tiled=True
            ).astype(jnp.float32),
        )
        shard_grads = sum_data(shard_grads)
        shard_total = shard_grads if shard_total is None else add_parts(shard_total, shard_grads)
        minor_total = minor_grads if minor_total is None else add_parts(minor_total, minor_grads)
    minor_sums = lax.psum(
        (minor_total[0], minor_total[1], minor_total[2], minor_total[3], minor_total[4]),
        ("dp", "fsdp"),
    )
    block_out = jnp.stack(out_rows, axis=0)
    d_tokens = jnp.stack(grad_rows, axis=0)
    d_condition = jnp.stack(cond_rows, axis=0)
    return (
        block_out,
        d_tokens,
        d_condition,
        shard_total[0],
        minor_sums[0],
        shard_total[1],
        minor_sums[1],
        minor_sums[2],
        minor_sums[3],
        shard_total[2],
        minor_sums[4],
        shard_total[3],
        shard_total[4],
        shard_total[5],
    )


def solution(mesh):
    placed = (
        P(None, ("dp", "fsdp"), None),
        P(None, ("dp", "fsdp"), None, None),
        P(None, ("dp", "fsdp"), None),
        P("fsdp", None),
        P(),
        P("fsdp", None),
        P(),
        P(),
        P(),
        P("fsdp", None),
        P(),
        P("fsdp", None),
        P("fsdp", None),
        P("fsdp", None),
        P(None, ("dp", "fsdp"), None),
    )
    dp, fsdp = mesh.shape["dp"], mesh.shape["fsdp"]
    if (dp, fsdp) == (8, 4):
        shards = partial(shards_fast, dp=dp, fsdp=fsdp)
    else:
        shards = shards_plain
    return jax.shard_map(
        shards,
        mesh=mesh,
        in_specs=placed,
        out_specs=(
            P(None, ("dp", "fsdp"), None),
            P(None, ("dp", "fsdp"), None),
            P(None, ("dp", "fsdp"), None, None),
            P("fsdp", None),
            P(),
            P("fsdp", None),
            P(),
            P(),
            P(),
            P("fsdp", None),
            P(),
            P("fsdp", None),
            P("fsdp", None),
            P("fsdp", None),
        ),
        check_vma=False,
    )
```
